256 devices in a mesh: depth: 8 (over z), board: 32 (over x, y, core).
Axes of the slice: x: 4, y: 4, z: 8, core: 2. Of those that a mesh axis runs over, the one named last changes fastest.
Arguments:
- root_reach: float32 [32, 1326], P('board'), may hold values from 0.05 to 1
- opp_strat: float32 [32, 8, 16, 1326], P('board', 'depth'), may hold values from 0.55 to 1
- own_strat: float32 [32, 8, 16, 1326], P('board', 'depth'), may hold values from 0.55 to 1
- parent: int32 [8, 16], P('depth'), may hold values from 0 to 15
- pot: float32 [32, 8, 16], P('board', 'depth'), may hold values from 1 to 8
- hand_cards: int32 [1326, 2], replicated, may hold values from 0 to 51, as said below
- river_card: int32 [32, 26], P('board'), may hold values from 0 to 51, as said below
- board_owner: int32 [32, 26], P('board'), may hold values from 0 to 31
- board_slot: int32 [32, 26], P('board'), may hold values from 0 to 1, as said below
- river_strength: float32 [32, 32, 2, 1326], P('board'), may hold values from -6 to 6
Outputs:
- node_value: float32 [32, 8, 16, 1326], P('board', 'depth')
The draws below stay inside these ranges and needn't reach their ends.
Inputs may be any that keep to these rules, and one draw needn't show every extreme that they name: `hand_cards`: each row holds two different cards, the lower first; no two rows are the same hand. `river_card`: the river cards of one front are distinct. Within one row of board_owner and board_slot the pairs are distinct; in every row some owner takes all 2 slots.
All inputs are finite; a program needn't handle non-finite values.
Results may differ from the reference program's by a relative error of at most 0.0003.
Values may be sent and summed in bfloat16 or wider, within the bound.
No kernel may reach another device: no remote copies, remote signals or barrier semaphores. Data moves between devices by JAX's collectives and lax.ppermute only.
A program may use at most 64 MiB of HBM per device.

```python
import math
import jax
import jax.numpy as jnp
import numpy as np
from jax import lax

HANDS = 1326
NODES = 16
RIVERS = 26
LEVELS = 8
FRONTS = 32
CAPACITY = 2
N_BOARD = 32


def hand_pairs():
    lower_card, second = np.triu_indices(52, 1)
    return np.stack([lower_card, second], 1).astype(np.int32)


def draw_hand_cards(key, part):
    ordering = jax.random.permutation(key, 1326)[:HANDS]
    return jnp.asarray(hand_pairs())[ordering]


def draw_river_card(key, part):
    front_keys = jax.random.split(key, FRONTS)
    picked = jax.vmap(lambda one_key: jax.random.permutation(one_key, 52)[:RIVERS])(front_keys)
    return picked.astype(jnp.int32)


def owner_lists(key):
    base_key = jax.random.fold_in(key, 7)
    total_slots = N_BOARD * CAPACITY
    hot_count = max(1, min(N_BOARD // 4, RIVERS // CAPACITY))
    hot_rank = jax.random.permutation(jax.random.fold_in(base_key, 1), N_BOARD)
    is_hot = (hot_rank < hot_count).astype(jnp.int32)
    noise = jax.random.randint(jax.random.fold_in(base_key, 2), (N_BOARD, total_slots), 0, 2 ** 15)
    candidate = jnp.arange(total_slots, dtype=jnp.int32)
    owner_of = candidate // CAPACITY
    score = (is_hot[owner_of][None, :] * 2 ** 15 + noise) * total_slots + candidate[None, :]
    top_scores, chosen = lax.top_k(score, RIVERS)
    row_keys = jax.random.split(jax.random.fold_in(base_key, 3), N_BOARD)
    shuffles = jax.vmap(lambda one_key: jax.random.permutation(one_key, RIVERS))(row_keys)
    chosen = jnp.take_along_axis(chosen, shuffles, axis=1)
    return ((chosen // CAPACITY).astype(jnp.int32), (chosen % CAPACITY).astype(jnp.int32))


def draw_board_owner(key, part):
    return owner_lists(key)[0]


def draw_board_slot(key, part):
    return owner_lists(key)[1]


def plant(values, key, low, top_value):
    extent = values.shape
    place = [jax.random.randint(jax.random.fold_in(key, axis), (), 0, extent[axis]) for axis in range(len(extent))]
    values = values.at[tuple(place)].set(low)
    longest = extent.index(max(extent))
    place[longest] = (place[longest] + 1) % extent[longest]
    return values.at[tuple(place)].set(top_value)


def block_scale(stream_key, shape, cuts, low, top_value):
    def one(dim, shards_of):
        draws = jax.random.uniform(jax.random.fold_in(jax.random.fold_in(stream_key, 6), dim), (shards_of,), jnp.float32, low / len(cuts), top_value / len(cuts))
        return jnp.repeat(jnp.exp(draws), shape[dim] // shards_of).reshape((-1,) + (1,) * (len(shape) - dim - 1))

    factor_of = one(*cuts[0])
    for cut in cuts[1:]:
        factor_of = factor_of * one(*cut)
    return factor_of


def centred(key, extent, width, limit, shards=(), kind=jnp.bfloat16):
    array = jax.random.normal(key, extent, jnp.float32) * width
    if len(shards) > 0:
        array = block_scale(key, extent, shards, -0.22, 0.18) * array
    return jnp.clip(array, min=-limit, max=limit).astype(kind)


def setup_inputs(seed: int = 0) -> dict:
    splits = jax.random.split(jax.random.key(seed), 11)
    root_reach = jnp.clip(0.05 + 0.95 * jax.random.uniform(splits[0], (FRONTS, HANDS), jnp.float32) ** block_scale(splits[0], (FRONTS, HANDS), ((0, 32),), -0.2, 0.2), 0.05, 1.0)
    opp_strat = jnp.clip(jnp.exp(math.log(1.0) - 0.597837 * jax.random.uniform(splits[1], (FRONTS, LEVELS, NODES, HANDS), jnp.float32) ** block_scale(splits[1], (FRONTS, LEVELS, NODES, HANDS), ((0, 32), (1, 8)), -0.2, 0.2)), 0.55, 1.0)
    own_strat = jnp.clip(jnp.exp(math.log(1.0) - 0.597837 * jax.random.uniform(splits[2], (FRONTS, LEVELS, NODES, HANDS), jnp.float32) ** block_scale(splits[2], (FRONTS, LEVELS, NODES, HANDS), ((0, 32), (1, 8)), -0.2, 0.2)), 0.55, 1.0)
    parent = plant(jax.random.randint(splits[3], (LEVELS, NODES), 0, NODES), jax.random.fold_in(splits[3], 1), 0, NODES - 1).astype(jnp.int32)
    pot = jnp.clip(jnp.exp(math.log(8.0) - 2.0794415 * jax.random.uniform(splits[4], (FRONTS, LEVELS, NODES), jnp.float32) ** block_scale(splits[4], (FRONTS, LEVELS, NODES), ((0, 32), (1, 8)), -0.2, 0.2)), 1.0, 8.0)
    hand_cards = draw_hand_cards(jax.random.fold_in(splits[10], 71), 0)
    river_card = draw_river_card(jax.random.fold_in(splits[10], 71), 0)
    board_owner = draw_board_owner(jax.random.fold_in(splits[10], 71), 0)
    board_slot = draw_board_slot(jax.random.fold_in(splits[10], 71), 0)
    river_strength = centred(splits[9], (N_BOARD, FRONTS, CAPACITY, HANDS), 1.0, 6.0, ((0, 32),), jnp.float32)
    return dict(root_reach=root_reach, opp_strat=opp_strat, own_strat=own_strat, parent=parent, pot=pot, hand_cards=hand_cards, river_card=river_card, board_owner=board_owner, board_slot=board_slot, river_strength=river_strength)


def reference(root_reach, opp_strat, own_strat, parent, pot, hand_cards, river_card, board_owner, board_slot, river_strength):
    deck = jnp.arange(52, dtype=jnp.int32)
    onehot_cards = ((hand_cards[:, 0:1] == deck[None, :]) | (hand_cards[:, 1:2] == deck[None, :])).astype(jnp.float32)
    intersection = jnp.dot(onehot_cards, onehot_cards.T, preferred_element_type=jnp.float32)
    compatible = (intersection < 0.5).astype(jnp.float32)
    reach_rows = jnp.broadcast_to(root_reach[:, None, :], (FRONTS, NODES, HANDS))
    stacked = []
    for level_index in range(LEVELS):
        reach_rows = opp_strat[:, level_index] * jnp.take(reach_rows, parent[level_index], axis=1)
        stacked.append(reach_rows)
    reach_all = jnp.stack(stacked, axis=1)

    def one_front(inputs):
        front_index, reach_front, rivers_row, owner_row, slot_row = inputs

        def one_river(total, river_inputs):
            river, owner, slot = river_inputs
            strength = river_strength[owner, front_index, slot]
            missing = ((hand_cards[:, 0] != river) & (hand_cards[:, 1] != river)).astype(jnp.float32)
            rounded = (reach_front * missing[None, None, :]).astype(jnp.bfloat16)
            board_reach = lax.optimization_barrier(rounded).astype(jnp.float32).reshape(LEVELS * NODES, HANDS)
            sign_table = jnp.sign(strength[:, None] - strength[None, :]) * compatible
            result = jnp.dot(board_reach, sign_table.T, preferred_element_type=jnp.float32)
            return total + missing[None, :] * result, None

        start = jnp.zeros((LEVELS * NODES, HANDS), jnp.float32)
        total, unused = lax.scan(one_river, start, (rivers_row, owner_row, slot_row))
        return total.reshape(LEVELS, NODES, HANDS)

    fronts_index = jnp.arange(FRONTS, dtype=jnp.int32)
    summed = lax.map(one_front, (fronts_index, reach_all, river_card, board_owner, board_slot))
    showdown = pot[:, :, :, None] / (HANDS * RIVERS) * summed
    carried = jnp.zeros((FRONTS, NODES, HANDS), jnp.float32)
    values = [None] * LEVELS
    for level_index in reversed(range(LEVELS)):
        node_value = showdown[:, level_index] + carried
        values[level_index] = node_value
        weighted = own_strat[:, level_index] * node_value
        selector = (parent[level_index][:, None] == jnp.arange(NODES, dtype=jnp.int32)[None, :]).astype(jnp.float32)
        carried = jnp.einsum("km,fkh->fmh", selector, weighted, precision=lax.Precision.HIGHEST)
    return jnp.stack(values, axis=1)
```

```python
import jax
import jax.numpy as jnp
from jax import lax
from jax.experimental import pallas as pl
from jax.experimental.pallas import tpu as pltpu
from jax.sharding import PartitionSpec as P

LANES = 128
SCALE = 2.0**124
DEAD = 2.0**127
UNIT = 2.0**-25
LOW = 0.55
SPAN = 0.45
STEPS = 65535.0


def padded(n, to=LANES):
    return -(-n // to) * to


def pieces(x):
    first = x.astype(jnp.bfloat16)
    rest = x - first.astype(jnp.float32)
    second = rest.astype(jnp.bfloat16)
    third = (rest - second.astype(jnp.float32)).astype(jnp.bfloat16)
    return jnp.concatenate([first, second, third], axis=0)


def table_kernel(owner, slot, river, strengths, cards, compatible, table, rows, wide):
    rivers = owner.shape[1]
    hands = strengths.shape[2]
    width = rows.shape[1]
    blocks = width // LANES
    rows[...] = jnp.zeros(rows.shape, jnp.float32)
    first, second = cards[0:1, :], cards[1:2, :]
    dead_count = jnp.zeros((1, width), jnp.float32)
    for r in range(rivers):
        rows[r : r + 1, 0:hands] = strengths[owner[0, r], pl.ds(slot[0, r], 1), :] * SCALE
        card = river[0, r]
        dead = (first == card) | (second == card)
        rows[r : r + 1, :] = jnp.where(dead, DEAD, rows[r : r + 1, :])
        dead_count = dead_count + dead.astype(jnp.float32)
    rows[rivers : rivers + 1, :] = dead_count * UNIT

    def block(b, carry):
        at = pl.multiple_of(b * LANES, LANES)
        columns = rows[:, pl.ds(at, LANES)].T
        for r in range(rivers + 1):
            wide[r] = jnp.broadcast_to(columns[:, r : r + 1], (LANES, LANES))

        def tile(j, carry):
            to = pl.multiple_of(j * LANES, LANES)
            total = (rows[rivers : rivers + 1, pl.ds(to, LANES)] - wide[rivers]).astype(jnp.bfloat16)
            for r in range(rivers):
                apart = (wide[r] - rows[r : r + 1, pl.ds(to, LANES)]).astype(jnp.bfloat16)
                apart = jnp.maximum(apart, jnp.bfloat16(-UNIT))
                total = total + jnp.minimum(apart, jnp.bfloat16(UNIT))
            fits = compatible[pl.ds(at, LANES), pl.ds(to, LANES)]
            table[pl.ds(at, LANES), pl.ds(to, LANES)] = total * jnp.bfloat16(1.0 / UNIT) * fits
            return carry

        return lax.fori_loop(b, blocks, tile, carry)

    lax.fori_loop(0, blocks, block, 0)


def tree_kernel(level, table, shared, root, out, reach_rows, values, *, hands, scale):
    levels = shared.shape[0]
    nodes = shared.shape[1] // 2
    width = table.shape[0]
    blocks = width // LANES
    lane = lax.broadcasted_iota(jnp.int32, (nodes, 3 * nodes), 1)
    live = lax.broadcasted_iota(jnp.int32, (nodes, width), 1) < hands

    def decoded(coded):
        value = (coded.astype(jnp.float32) + 32768.0) * (SPAN / STEPS) + LOW
        return jnp.where(live, value, 0.0)

    def chosen(l):
        parent = shared[l, 0:nodes, hands : hands + 1].astype(jnp.int32)
        return (lane % nodes == parent).astype(jnp.bfloat16)

    current = decoded(shared[0, 0:nodes, :]) * root[...]
    reach_rows[0:nodes, :] = current.astype(jnp.bfloat16)
    for l in range(1, levels):
        above = jnp.dot(chosen(l), pieces(current), preferred_element_type=jnp.float32)
        current = decoded(shared[l, 0:nodes, :]) * above
        reach_rows[l * nodes : (l + 1) * nodes, :] = current.astype(jnp.bfloat16)

    values[...] = jnp.zeros(values.shape, jnp.float32)
    for b in range(blocks):
        at, end = b * LANES, (b + 1) * LANES
        values[:, at:end] += lax.dot_general(
            reach_rows[:, at:], table[at:end, at:], (((1,), (1,)), ((), ())),
            preferred_element_type=jnp.float32,
        )
        if end < width:
            values[:, end:] -= jnp.dot(
                reach_rows[:, at:end], table[at:end, end:], preferred_element_type=jnp.float32
            )

    carried = jnp.zeros((nodes, width), jnp.float32)
    for l in reversed(range(levels)):
        high = shared[l, 0:nodes, hands + 1 : hands + 2].astype(jnp.float32)
        low = shared[l, 0:nodes, hands + 2 : hands + 3].astype(jnp.float32)
        pot = (high + low * 2.0**-15) * 2.0**-12
        value = values[l * nodes : (l + 1) * nodes, :] * (pot * scale) + carried

        @pl.when(level[0] == l)
        def _():
            out[...] = value[:, 0:hands]

        if l > 0:
            weighted = decoded(shared[l, nodes : 2 * nodes, :]) * value
            carried = sum_to_parents(chosen(l), weighted, nodes)


def sum_to_parents(selector, weighted, nodes):
    picks = selector[:, 0:nodes].astype(jnp.float32).T.astype(jnp.bfloat16)
    picks = jnp.concatenate([picks, picks, picks], axis=1)
    return jnp.dot(picks, pieces(weighted), preferred_element_type=jnp.float32)


def coded(x, width):
    steps = jnp.round((x - LOW) * (STEPS / SPAN)) - 32768.0
    steps = jnp.clip(steps, -32768.0, 32767.0).astype(jnp.int16)
    return jnp.pad(steps, ((0, 0), (0, width - x.shape[1])))


def body(
    root_reach,
    opp_strat,
    own_strat,
    parent,
    pot,
    hand_cards,
    river_card,
    board_owner,
    board_slot,
    river_strength,
):
    hands = root_reach.shape[1]
    nodes = opp_strat.shape[2]
    rivers = river_card.shape[1]
    width = padded(hands + 3)
    levels = lax.axis_size("depth")

    fetched = lax.all_to_all(river_strength[0], "board", split_axis=0, concat_axis=0, tiled=True)

    scaled_pot = pot[0, 0] * 4096.0
    high = jnp.floor(scaled_pot)
    low = (scaled_pot - high) * 32768.0
    extra = jnp.stack([parent[0].astype(jnp.float32), high, low], axis=1).astype(jnp.int16)
    opp_coded = coded(opp_strat[0, 0], width)
    opp_coded = lax.dynamic_update_slice(opp_coded, extra, (0, hands))
    message = jnp.concatenate([opp_coded, coded(own_strat[0, 0], width)], axis=0)
    copies = jnp.broadcast_to(message, (levels, *message.shape))
    shared = lax.all_to_all(copies, "depth", split_axis=0, concat_axis=0, tiled=True)

    cards = jnp.pad(hand_cards.T, ((0, 0), (0, width - hands)), constant_values=-1)
    held = cards[None, :, :] == jnp.arange(64, dtype=jnp.int32)[:, None, None]
    onehot = (held[:, 0] | held[:, 1]).astype(jnp.bfloat16)
    together = lax.dot_general(
        onehot, onehot, (((0,), (0,)), ((), ())), preferred_element_type=jnp.float32
    )
    compatible = (together < 0.5).astype(jnp.bfloat16)

    smem = pl.BlockSpec(memory_space=pltpu.SMEM)
    vmem = pl.BlockSpec(memory_space=pltpu.VMEM)
    table = pl.pallas_call(
        table_kernel,
        out_shape=jax.ShapeDtypeStruct((width, width), jnp.bfloat16),
        in_specs=[smem, smem, smem, vmem, vmem, vmem],
        out_specs=vmem,
        scratch_shapes=[
            pltpu.VMEM((32, width), jnp.float32),
            pltpu.VMEM((rivers + 1, LANES, LANES), jnp.float32),
        ],
        name="sign_table",
    )(board_owner, board_slot, river_card, fetched, cards, compatible)

    root = jnp.pad(root_reach, ((0, 0), (0, width - hands)))
    level = lax.axis_index("depth").astype(jnp.int32).reshape(1)

    def tree(*refs):
        tree_kernel(*refs, hands=hands, scale=1.0 / (hands * rivers))

    node_value = pl.pallas_call(
        tree,
        out_shape=jax.ShapeDtypeStruct((nodes, hands), jnp.float32),
        in_specs=[smem, vmem, vmem, vmem],
        out_specs=vmem,
        scratch_shapes=[
            pltpu.VMEM((levels * nodes, width), jnp.bfloat16),
            pltpu.VMEM((levels * nodes, width), jnp.float32),
        ],
        name="tree_values",
    )(level, table, shared, root)
    return node_value[None, None]


def solution(mesh):
    placed = (
        P("board", None),
        P("board", "depth", None, None),
        P("board", "depth", None, None),
        P("depth", None),
        P("board", "depth", None),
        P(),
        P("board", None),
        P("board", None),
        P("board", None),
        P("board", None, None, None),
    )
    return jax.shard_map(
        body, mesh=mesh, in_specs=placed, out_specs=P("board", "depth", None, None), check_vma=False
    )
```
